512 devices in a mesh: sub: 128 (over y, z, core), freq: 4 (over x).
Axes of the slice: x: 4, y: 8, z: 8, core: 2. Of those that a mesh axis runs over, the one named last changes fastest.
Arguments:
- response: bfloat16 [4, 1536, 96, 256], P('freq', 'sub'), may hold values from -6 to 6
- measured: bfloat16 [4, 12288, 256], P('freq', 'sub'), may hold values from -6 to 6
- sensor_owner: int32 [12288], P('sub'), may hold values from 0 to 127, as said below
- sensor_row: int32 [12288], P('sub'), may hold values from 0 to 1151
- adj_diag: bfloat16 [4, 1536, 2, 96, 96], P('freq', 'sub')
- adj_off: bfloat16 [4, 1536, 5, 2, 96, 96], P('freq', 'sub')
- block_cols: int32 [1536, 5], P('sub'), may hold values from 0 to 13, as said below
- precond: bfloat16 [4, 1536, 2, 96, 96], P('freq', 'sub')
- stiff_deriv: bfloat16 [1536, 96, 96], P('sub'), may hold values from -0.625 to 0.625
Outputs:
- adjoint: bfloat16 [4, 1536, 96, 256], P('freq', 'sub')
- gradient: float32 [1536], P('sub')
The draws below stay inside these ranges and needn't reach their ends.
Inputs may be any that keep to these rules, and one draw needn't show every extreme that they name: `sensor_owner`: among the 96 channels held by one index of sub, no subdomain is named more than 3 times, and one subdomain is named exactly 3 times by the channels of every index of sub. `block_cols`: in every subdomain some block row has a coupling tile with column 0 and some has one with column 13.
All inputs are finite; a program needn't handle non-finite values.
Results may differ from the reference program's by a relative error of at most 0.0061.
Values may be sent and summed in bfloat16 or wider, within the bound.
No kernel may reach another device: no remote copies, remote signals or barrier semaphores. Data moves between devices by JAX's collectives and lax.ppermute only.
A program may use at most 64 MiB of HBM per device.

```python
import math
import jax
import jax.numpy as jnp
from jax import lax

BS = 96
R = 128
NBD = 12
NNB = 5
SWEEPS = 3
SENS_DEV = 96
FREQ = 4
NB = 1536
NSENS = 12288
CAP = 3


def tile_noise(rng_key, shape):
    return jax.random.normal(rng_key, shape, jnp.float32)


def diag_level(rng_key):
    return jax.random.uniform(jax.random.fold_in(rng_key, 11), (FREQ, NB, BS), jnp.float32, 2.0, 4.0)


def draw_adj_diag(key, part):
    level = diag_level(key)
    noise = tile_noise(jax.random.fold_in(key, 12), (FREQ, NB, 2, BS, BS))
    identity = jnp.eye(BS, dtype=jnp.float32)
    real_part = noise[:, :, 0] * (1.0 / math.sqrt(BS)) + level[..., None] * identity
    imag_part = noise[:, :, 1] * (0.5 / math.sqrt(BS)) + 0.4 * identity
    return jnp.stack([real_part, imag_part], axis=2).astype(jnp.bfloat16)


def draw_precond(key, part):
    level = diag_level(key)
    noise = tile_noise(jax.random.fold_in(key, 13), (FREQ, NB, 2, BS, BS))
    identity = jnp.eye(BS, dtype=jnp.float32)
    denominator = level * level + 0.16
    real_part = (level / denominator)[..., None] * identity + noise[:, :, 0] * (0.1 / math.sqrt(BS))
    imag_part = (-0.4 / denominator)[..., None] * identity + noise[:, :, 1] * (0.05 / math.sqrt(BS))
    return jnp.stack([real_part, imag_part], axis=2).astype(jnp.bfloat16)


def draw_adj_off(key, part):
    noise = tile_noise(jax.random.fold_in(key, 14), (FREQ, NB, NNB, 2, BS, BS))
    factors = jnp.array([0.5, 0.25], jnp.float32)[:, None, None] * (1.0 / math.sqrt(BS))
    return (noise * factors).astype(jnp.bfloat16)


def draw_block_cols(key, part):
    subdomain_count = NB // NBD
    columns = jax.random.randint(jax.random.fold_in(key, 15), (subdomain_count, NBD, NNB), 0, NBD + 2, jnp.int32)
    columns = columns.at[:, 0, 0].set(0)
    columns = columns.at[:, NBD - 1, 0].set(NBD + 1)
    return columns.reshape(NB, NNB)


def draw_sensor_owner(key, part):
    subdomain_count = NSENS // SENS_DEV
    hot_owner = jax.random.randint(jax.random.fold_in(key, 16), (), 0, subdomain_count, jnp.int32)
    offsets = jax.random.randint(jax.random.fold_in(key, 17), (subdomain_count, 1), 0, subdomain_count - 1, jnp.int32)
    positions = jnp.arange(SENS_DEV, dtype=jnp.int32)[None, :]
    spread = (positions - CAP + offsets) % (subdomain_count - 1)
    owners = jnp.where(positions < CAP, hot_owner, (hot_owner + 1 + spread) % subdomain_count)
    perm_keys = jax.random.split(jax.random.fold_in(key, 18), subdomain_count)
    orders = jax.vmap(lambda perm_key: jax.random.permutation(perm_key, SENS_DEV))(perm_keys)
    owners = jnp.take_along_axis(owners, orders.astype(jnp.int32), axis=1)
    return owners.reshape(NSENS).astype(jnp.int32)


def plant(drawn, stream_key, low, top_value):
    longest = drawn.shape.index(max(drawn.shape))
    spots = []
    for shift in (0, 1):
        where = [jax.random.randint(jax.random.fold_in(stream_key, axis), (), 0, length) for axis, length in enumerate(drawn.shape)]
        where[longest] = (where[longest] + shift) % drawn.shape[longest]
        spots.append(tuple(where))
    return drawn.at[spots[0]].set(low).at[spots[1]].set(top_value)


def shard_levels(own_key, shape, cuts, least, largest):
    def one(axis_at, blocks):
        heights = jax.random.uniform(jax.random.fold_in(jax.random.fold_in(own_key, 6), axis_at), (blocks,), jnp.float32, least / len(cuts), largest / len(cuts))
        return jnp.repeat(jnp.exp(heights), shape[axis_at] // blocks).reshape((-1,) + (1,) * (len(shape) - axis_at - 1))

    factor_of = one(*cuts[0])
    for cut in cuts[1:]:
        factor_of = factor_of * one(*cut)
    return factor_of


def bell_draw(stream_key, shape, scale, reach, pieces=(), kind=jnp.bfloat16):
    values = jax.random.normal(stream_key, shape, jnp.float32) * scale
    if len(pieces) > 0:
        values = shard_levels(stream_key, shape, pieces, -0.22, 0.18) * values
    return jnp.clip(values, min=-reach, max=reach).astype(kind)


def setup_inputs(seed: int = 0) -> dict:
    key_of = jax.random.split(jax.random.key(seed), 10)
    return {
        "response": bell_draw(key_of[0], (FREQ, NB, BS, 2 * R), 1.0, 6.0, ((0, 4), (1, 128))),
        "measured": bell_draw(key_of[1], (FREQ, NSENS, 2 * R), 1.0, 6.0, ((0, 4), (1, 128))),
        "sensor_owner": draw_sensor_owner(jax.random.fold_in(key_of[9], 71), 0),
        "sensor_row": plant(jax.random.randint(key_of[3], (NSENS,), 0, NBD * BS), jax.random.fold_in(key_of[3], 1), 0, (NBD * BS) - 1).astype(jnp.int32),
        "adj_diag": draw_adj_diag(jax.random.fold_in(key_of[9], 71), 0),
        "adj_off": draw_adj_off(jax.random.fold_in(key_of[9], 71), 0),
        "block_cols": draw_block_cols(jax.random.fold_in(key_of[9], 71), 0),
        "precond": draw_precond(jax.random.fold_in(key_of[9], 71), 0),
        "stiff_deriv": bell_draw(key_of[8], (NB, BS, BS), BS ** -0.5, 0.625, ((0, 128),)),
    }


def complex_apply(tile_set, vectors):
    column_half = vectors.shape[-1] // 2
    real_part = jnp.einsum('bij,bjn->bin', tile_set[:, 0], vectors, precision=lax.Precision.HIGHEST)
    imag_part = jnp.einsum('bij,bjn->bin', tile_set[:, 1], vectors, precision=lax.Precision.HIGHEST)
    return jnp.concatenate([real_part[..., :column_half] - imag_part[..., column_half:], real_part[..., column_half:] + imag_part[..., :column_half]], axis=-1)

def coupled_apply(iterate, off_tiles, padded_index):
    subdomain_count = NB // NBD
    col_count = iterate.shape[-1]
    column_half = col_count // 2
    empty_zero_block = jnp.zeros((1, BS, col_count), jnp.bfloat16)
    padded = jnp.concatenate([empty_zero_block, iterate, empty_zero_block], axis=0)

    def per_sub(inputs_pair):
        tile_set, index_set = inputs_pair
        near_blocks = padded[index_set].astype(jnp.float32)
        tile_f32 = tile_set.astype(jnp.float32)
        real_part = jnp.einsum('bkij,bkjn->bin', tile_f32[:, :, 0], near_blocks, precision=lax.Precision.HIGHEST)
        imag_part = jnp.einsum('bkij,bkjn->bin', tile_f32[:, :, 1], near_blocks, precision=lax.Precision.HIGHEST)
        return jnp.concatenate([real_part[..., :column_half] - imag_part[..., column_half:], real_part[..., column_half:] + imag_part[..., :column_half]], axis=-1)
    result = lax.map(per_sub, (off_tiles.reshape(subdomain_count, NBD, NNB, 2, BS, BS), padded_index.reshape(subdomain_count, NBD, NNB)))
    return result.reshape(NB, BS, col_count)

def reference(response, measured, sensor_owner, sensor_row, adj_diag, adj_off, block_cols, precond, stiff_deriv):
    col_count = 2 * R
    flat_index = (sensor_owner * (NBD * BS) + sensor_row).astype(jnp.int32)
    leading_block = jnp.arange(NB, dtype=jnp.int32) // NBD * NBD
    padded_index = (leading_block[:, None] + block_cols).astype(jnp.int32)
    grad_scale = 1.0 / math.sqrt(2 * BS * R)
    stiff_f32 = stiff_deriv.astype(jnp.float32)
    adjoints = []
    gradient = jnp.zeros((NB,), jnp.float32)
    for freq_step in range(FREQ):
        resp_now = response[freq_step]
        flat_resp = resp_now.reshape(NB * BS, col_count).astype(jnp.float32)
        misfit = flat_resp[flat_index] - measured[freq_step].astype(jnp.float32)
        load_rhs = jnp.zeros((NB * BS, col_count), jnp.float32).at[flat_index].add(misfit).reshape(NB, BS, col_count)
        diag_f32 = adj_diag[freq_step].astype(jnp.float32)
        prec_f32 = precond[freq_step].astype(jnp.float32)
        load_low = lax.optimization_barrier(load_rhs.astype(jnp.bfloat16)).astype(jnp.float32)
        adjoint = complex_apply(prec_f32, load_low)
        for jacobi_sweep_step in range(SWEEPS - 1):
            iterate = lax.optimization_barrier(adjoint.astype(jnp.bfloat16))
            applied = complex_apply(diag_f32, iterate.astype(jnp.float32)) + coupled_apply(iterate, adj_off[freq_step], padded_index)
            update = lax.optimization_barrier((load_rhs - applied).astype(jnp.bfloat16)).astype(jnp.float32)
            adjoint = adjoint + complex_apply(prec_f32, update)
        adjoints.append(adjoint.astype(jnp.bfloat16))
        stiff_resp = jnp.einsum('bij,bjn->bin', stiff_f32, resp_now.astype(jnp.float32), precision=lax.Precision.HIGHEST)
        gradient = gradient + lax.optimization_barrier(jnp.sum(adjoint * stiff_resp, axis=(1, 2))) * grad_scale
    return (jnp.stack(adjoints), gradient)
```

```python
import functools
import math

import jax
import jax.numpy as jnp
from jax import lax
from jax.experimental import pallas as pl
from jax.experimental.pallas import tpu as pltpu
from jax.sharding import PartitionSpec as P

SLOTS = 4
VMEM_LIMIT = 48 * 1024 * 1024

F32 = jnp.float32
BF16 = jnp.bfloat16


def iota(shape, dim):
    return lax.broadcasted_iota(jnp.int32, shape, dim)


def complex_product(tile_pair, block):
    _, m, depth = tile_pair.shape
    half = block.shape[-1] // 2
    both = jnp.dot(tile_pair.reshape(2 * m, depth), block, preferred_element_type=F32)
    return combine(both, m, half)


def combine(both, m, half):
    real_part = both[:m, :half] - both[m:, half:]
    imag_part = both[:m, half:] + both[m:, :half]
    return real_part, imag_part


def pack_kernel(rows_per, owner_ref, row_ref, measured_ref, out_ref):
    count = measured_ref.shape[0]
    slots_all = out_ref.shape[0]
    owner = owner_ref[...]
    row = row_ref[...]
    code = (owner * 2048 + row).astype(F32)
    lanes = jnp.broadcast_to(jnp.pad(code, ((0, 0), (0, 128 - count))), (128, 128))
    code_col = jnp.transpose(lanes)[:count, :count].astype(jnp.int32)
    owner_col = code_col >> 11
    row_col = code_col & 2047
    same = jnp.broadcast_to(owner, (count, count)) == owner_col
    sub = iota((count, count), 0)
    lane = iota((count, count), 1)
    rank_row = jnp.sum(jnp.where(same & (sub < lane), 1, 0), axis=0, keepdims=True)
    rank_col = jnp.sum(jnp.where(same & (lane < sub), 1, 0), axis=1, keepdims=True)
    place = iota((slots_all, count), 0)
    here = (place >> 2) == owner
    slot = place & 3
    pick = jnp.where(here & (slot == rank_row), 1.0, 0.0).astype(BF16)
    tell = jnp.where(here & (slot == SLOTS - 1), 1.0, 0.0).astype(BF16)
    width = iota((count, 128), 1)
    row_wide = jnp.broadcast_to(row_col[:, :1], (count, 128))
    block = row_wide // rows_per
    inner = row_wide - block * rows_per
    numbers = jnp.where(width == rank_col, block + 1, 0) + jnp.where(
        width == rank_col + SLOTS, inner, 0
    )
    numbers = numbers.astype(F32).astype(BF16)
    rows = jnp.dot(pick, measured_ref[...], preferred_element_type=F32)
    told = jnp.dot(tell, numbers, preferred_element_type=F32)
    half = rows.shape[-1] // 2
    out_ref[:, :half] = (rows[:, :half] + told).astype(BF16)
    out_ref[:, half:] = rows[:, half:].astype(BF16)


def load_kernel(recv_ref, resp_ref, prec_ref, load_ref, lam_ref, it_ref, first_ref, last_ref, place_ref):
    nb, m, cols = resp_ref.shape
    half = cols // 2
    places = recv_ref.shape[0]
    recv = recv_ref[...]
    turned = jnp.transpose(recv[:, :half].astype(F32)).astype(BF16)
    lane = iota((m, half), 1)
    slot = iota((m, places), 1) & 3
    where_row = jnp.full((m, places), -1.0, F32)
    for s in range(SLOTS - 1):
        weights = jnp.where(lane == s, m, 0) + jnp.where(lane == s + SLOTS, 1, 0)
        told = jnp.dot(weights.astype(F32).astype(BF16), turned, preferred_element_type=F32)
        told = pltpu.roll(told, places + s - (SLOTS - 1), 1)
        where_row = jnp.where(slot == s, told - m, where_row)
    place_ref[...] = where_row.astype(jnp.int32) - iota((m, places), 0)
    ones = jnp.ones((places, half), BF16)

    def one(b):
        hit = jnp.where(place_ref[...] == b * m, 1.0, 0.0).astype(BF16)
        summed = jnp.dot(hit, recv, preferred_element_type=F32)
        number = jnp.dot(hit, ones, preferred_element_type=F32)
        resp = resp_ref[b].astype(F32)
        load_re = number * resp[:, :half] - summed[:, :half]
        load_im = number * resp[:, half:] - summed[:, half:]
        load = jnp.concatenate([load_re, load_im], axis=1)
        load_ref[b] = load
        lam_re, lam_im = complex_product(prec_ref[b], load.astype(BF16))
        lam = jnp.concatenate([lam_re, lam_im], axis=1)
        lam_ref[b] = lam
        it_ref[b] = lam.astype(BF16)

    pl.loop(0, nb)(one)
    first_ref[...] = it_ref[0]
    last_ref[...] = it_ref[nb - 1]


def sweep_block(b, cols_ref, ext_ref, load_ref, lam_ref, diag_ref, off_ref, prec_ref):
    _, m, cols = load_ref.shape
    half = cols // 2
    near = off_ref.shape[1]
    both = jnp.dot(diag_ref[b].reshape(2 * m, m), ext_ref[b + 1], preferred_element_type=F32)
    for k in range(near):
        g = cols_ref[b * near + k]
        both += jnp.dot(off_ref[b, k].reshape(2 * m, m), ext_ref[g], preferred_element_type=F32)
    applied_re, applied_im = combine(both, m, half)
    load = load_ref[b]
    update = jnp.concatenate(
        [load[:, :half] - applied_re, load[:, half:] - applied_im], axis=1
    ).astype(BF16)
    step_re, step_im = complex_product(prec_ref[b], update)
    return lam_ref[b] + jnp.concatenate([step_re, step_im], axis=1)


def fill_ext(ext_ref, it_ref, low_ref, high_ref):
    nb = it_ref.shape[0]
    ext_ref[0] = low_ref[...]
    ext_ref[nb + 1] = high_ref[...]
    ext_ref[1 : nb + 1] = it_ref[...]


def sweep_kernel(
    cols_ref, it_ref, low_ref, high_ref, load_ref, lam_ref, diag_ref, off_ref, prec_ref,
    lam_out, it_out, first_ref, last_ref, ext_ref,
):
    nb = load_ref.shape[0]
    fill_ext(ext_ref, it_ref, low_ref, high_ref)

    def one(b):
        lam = sweep_block(b, cols_ref, ext_ref, load_ref, lam_ref, diag_ref, off_ref, prec_ref)
        lam_out[b] = lam
        it_out[b] = lam.astype(BF16)

    pl.loop(0, nb)(one)
    first_ref[...] = it_out[0]
    last_ref[...] = it_out[nb - 1]


def last_kernel(
    scale, cols_ref, it_ref, low_ref, high_ref, load_ref, lam_ref, diag_ref, off_ref, prec_ref,
    stiff_ref, resp_ref, adj_out, grad_out, ext_ref,
):
    nb = load_ref.shape[0]
    fill_ext(ext_ref, it_ref, low_ref, high_ref)
    grad_out[...] = jnp.zeros_like(grad_out)

    def one(b):
        lam = sweep_block(b, cols_ref, ext_ref, load_ref, lam_ref, diag_ref, off_ref, prec_ref)
        adj_out[b] = lam.astype(BF16)
        stiff_resp = jnp.dot(stiff_ref[b], resp_ref[b], preferred_element_type=F32)
        total = jnp.sum(lam * stiff_resp, axis=(0, 1), keepdims=True) * scale
        grad_out[...] += jnp.where(iota(grad_out.shape, 1) == b, total, 0.0)

    pl.loop(0, nb)(one)


def vmem(count):
    return [pl.BlockSpec(memory_space=pltpu.VMEM)] * count


def call(kernel, outs, n_in, smem=0, scratch=()):
    return pl.pallas_call(
        kernel,
        out_shape=outs,
        in_specs=[pl.BlockSpec(memory_space=pltpu.SMEM)] * smem + vmem(n_in),
        out_specs=tuple(vmem(len(outs))) if isinstance(outs, tuple) else vmem(1)[0],
        scratch_shapes=list(scratch),
        compiler_params=pltpu.CompilerParams(vmem_limit_bytes=VMEM_LIMIT),
    )


def halo(first, last, axis):
    count = lax.axis_size(axis)
    forward = [(i, i + 1) for i in range(count - 1)]
    backward = [(i + 1, i) for i in range(count - 1)]
    return lax.ppermute(last, axis, forward), lax.ppermute(first, axis, backward)


def shards(
    response, measured, sensor_owner, sensor_row, adj_diag, adj_off, block_cols, precond, stiff_deriv
):
    resp = response[0]
    diag, off, prec = adj_diag[0], adj_off[0], precond[0]
    nb, m, cols = resp.shape
    peers = lax.axis_size("sub")
    sensors = sensor_owner.shape[0]
    shape = jax.ShapeDtypeStruct
    packed = call(functools.partial(pack_kernel, m), shape((peers * SLOTS, cols), BF16), 3)(
        sensor_owner.reshape(1, sensors), sensor_row.reshape(1, sensors), measured[0]
    )
    recv = lax.all_to_all(packed.reshape(peers, SLOTS, cols), "sub", 0, 0, tiled=True)
    recv = recv.reshape(peers * SLOTS, cols)
    whole32, whole16 = shape((nb, m, cols), F32), shape((nb, m, cols), BF16)
    edge = shape((m, cols), BF16)
    load, lam, it, first, last = call(
        load_kernel, (whole32, whole32, whole16, edge, edge), 3, 0,
        [pltpu.VMEM((m, peers * SLOTS), jnp.int32)],
    )(
        recv, resp, prec
    )
    low, high = halo(first, last, "sub")
    near = block_cols.reshape(-1)
    ext = [pltpu.VMEM((nb + 2, m, cols), BF16)]
    lam, it, first, last = call(sweep_kernel, (whole32, whole16, edge, edge), 8, 1, ext)(
        near, it, low, high, load, lam, diag, off, prec
    )
    low, high = halo(first, last, "sub")
    scale = 1.0 / math.sqrt(m * cols)
    adjoint, grad = call(
        functools.partial(last_kernel, scale), (whole16, shape((1, nb), F32)), 10, 1, ext
    )(near, it, low, high, load, lam, diag, off, prec, stiff_deriv, resp)
    gradient = lax.psum(grad.reshape(nb), "freq")
    return (adjoint[None], gradient)


def solution(mesh):
    in_specs = (
        P("freq", "sub", None, None),
        P("freq", "sub", None),
        P("sub"),
        P("sub"),
        P("freq", "sub", None, None, None),
        P("freq", "sub", None, None, None, None),
        P("sub", None),
        P("freq", "sub", None, None, None),
        P("sub", None, None),
    )
    out_specs = (P("freq", "sub", None, None), P("sub"))
    return jax.shard_map(shards, mesh=mesh, in_specs=in_specs, out_specs=out_specs, check_vma=False)
```

```python
import functools
import math

import jax
import jax.numpy as jnp
from jax import lax
from jax.experimental import pallas as pl
from jax.experimental.pallas import tpu as pltpu
from jax.sharding import PartitionSpec as P

SLOTS = 4
VMEM_LIMIT = 16 * 1024 * 1024

F32 = jnp.float32
BF16 = jnp.bfloat16


def iota(shape, dim):
    return lax.broadcasted_iota(jnp.int32, shape, dim)


def split_product(both):
    m, half = both.shape[0] // 2, both.shape[1] // 2
    real_part = both[:m, :half] - both[m:, half:]
    imag_part = both[:m, half:] + both[m:, :half]
    return jnp.concatenate([real_part, imag_part], axis=1)


def stacked(tile_pair):
    return tile_pair.reshape(tile_pair.shape[0] * tile_pair.shape[1], tile_pair.shape[2])


def complex_product(tile_pair, block):
    return split_product(jnp.dot(stacked(tile_pair), block, preferred_element_type=F32))


def pack_kernel(rows_per, code_ref, measured_ref, out_ref):
    count = measured_ref.shape[0]
    slots_all = out_ref.shape[0]
    code = code_ref[...]
    owner = code.astype(jnp.int32) >> 11
    lanes = jnp.broadcast_to(jnp.pad(code, ((0, 0), (0, 128 - count))), (128, 128))
    code_col = jnp.transpose(lanes)[:count, :count].astype(jnp.int32)
    owner_col = code_col >> 11
    row_col = code_col & 2047
    same = jnp.broadcast_to(owner, (count, count)) == owner_col
    sub = iota((count, count), 0)
    lane = iota((count, count), 1)
    rank_row = jnp.sum(jnp.where(same & (sub < lane), 1, 0), axis=0, keepdims=True)
    rank_col = jnp.sum(jnp.where(same & (lane < sub), 1, 0), axis=1, keepdims=True)
    place = iota((slots_all, count), 0)
    here = (place >> 2) == owner
    slot = place & 3
    pick = jnp.where(here & (slot == rank_row), 1.0, 0.0).astype(BF16)
    tell = jnp.where(here & (slot == SLOTS - 1), 1.0, 0.0).astype(BF16)
    width = iota((count, 128), 1)
    row_wide = jnp.broadcast_to(row_col[:, :1], (count, 128))
    block = row_wide // rows_per
    inner = row_wide - block * rows_per
    numbers = jnp.where(width == rank_col, block + 1, 0) + jnp.where(
        width == rank_col + SLOTS, inner, 0
    )
    numbers = numbers.astype(F32).astype(BF16)
    rows = jnp.dot(pick, measured_ref[...], preferred_element_type=F32)
    told = jnp.dot(tell, numbers, preferred_element_type=F32)
    half = rows.shape[-1] // 2
    out_ref[:, :half] = (rows[:, :half] + told).astype(BF16)
    out_ref[:, half:] = rows[:, half:].astype(BF16)


def send_edges(parity, first, last, partner_ref, other_ref):
    even = parity == 0
    partner_ref[...] = jnp.where(even, last, first).astype(BF16)
    other_ref[...] = jnp.where(even, first, last).astype(BF16)


def take_edges(parity, partner_ref, other_ref, ext_ref):
    top = ext_ref.shape[0] - 1
    even = parity == 0
    ext_ref[jnp.where(even, top, 0)] = partner_ref[...]
    ext_ref[jnp.where(even, 0, top)] = other_ref[...]


def make_load(first, count, place_ref, recv, ones, resp_ref):
    m = place_ref.shape[0]
    half = recv.shape[1] // 2
    place = place_ref[...]
    hit = jnp.concatenate(
        [jnp.where(place == (first + i) * m, 1.0, 0.0).astype(BF16) for i in range(count)], axis=0
    )
    summed = jnp.dot(hit, recv, preferred_element_type=F32)
    number = jnp.dot(hit, ones, preferred_element_type=F32)
    loads = []
    for i in range(count):
        rows = slice(i * m, (i + 1) * m)
        resp = resp_ref[first + i].astype(F32)
        loads.append(
            jnp.concatenate([number[rows], number[rows]], axis=1) * resp - summed[rows]
        )
    return loads


def edge_kernel(parity_ref, recv_ref, resp_ref, prec_ref, place_ref, partner_ref, other_ref):
    nb, m, cols = resp_ref.shape
    half = cols // 2
    places = recv_ref.shape[0]
    recv = recv_ref[...]
    turned = jnp.transpose(recv[:, :half].astype(F32)).astype(BF16)
    lane = iota((m, half), 1)
    slot = iota((m, places), 1) & 3
    where_row = jnp.full((m, places), -1.0, F32)
    for s in range(SLOTS - 1):
        weights = jnp.where(lane == s, m, 0) + jnp.where(lane == s + SLOTS, 1, 0)
        told = jnp.dot(weights.astype(F32).astype(BF16), turned, preferred_element_type=F32)
        told = pltpu.roll(told, places + s - (SLOTS - 1), 1)
        where_row = jnp.where(slot == s, told - m, where_row)
    place_ref[...] = where_row.astype(jnp.int32) - iota((m, places), 0)
    ones = jnp.ones((places, half), BF16)
    edges = []
    for b in (0, nb - 1):
        load = make_load(b, 1, place_ref, recv, ones, resp_ref)[0]
        edges.append(complex_product(prec_ref[b], load.astype(BF16)))
    send_edges(parity_ref[0], *edges, partner_ref, other_ref)


def load_kernel(
    place_ref, recv_ref, resp_ref, prec_ref, stiff_ref, load_ref, lam_ref, ext_ref, stiff_out
):
    nb, m, cols = resp_ref.shape
    recv = recv_ref[...]
    ones = jnp.ones((recv.shape[0], cols // 2), BF16)
    group = 4 if nb % 4 == 0 else 1
    for first in range(0, nb, group):
        loads = make_load(first, group, place_ref, recv, ones, resp_ref)
        for i, load in enumerate(loads):
            b = first + i
            load_ref[b] = load
            lam = complex_product(prec_ref[b], load.astype(BF16))
            lam_ref[b] = lam
            ext_ref[b + 1] = lam.astype(BF16)
    for b in range(nb):
        stiff_out[b] = jnp.dot(stiff_ref[b], resp_ref[b], preferred_element_type=F32)


def sweep_blocks(blocks, cols_ref, ext_ref, load_ref, lam_ref, diag_ref, off_ref, prec_ref):
    near = off_ref.shape[1]
    updates = []
    for b in blocks:
        tiles = [stacked(diag_ref[b])] + [stacked(off_ref[b, k]) for k in range(near)]
        parts = [ext_ref[b + 1]] + [ext_ref[cols_ref[b * near + k]] for k in range(near)]
        both = None
        for i in range(0, near + 1, 2):
            part = jnp.dot(
                jnp.concatenate(tiles[i : i + 2], axis=1),
                jnp.concatenate(parts[i : i + 2], axis=0),
                preferred_element_type=F32,
            )
            both = part if both is None else both + part
        updates.append((load_ref[b] - split_product(both)).astype(BF16))
    for b, update in zip(blocks, updates):
        yield b, lam_ref[b] + complex_product(prec_ref[b], update)


def sweep_edge_kernel(
    parity_ref, cols_ref, from_partner, from_other, load_ref, lam_ref, diag_ref, off_ref, prec_ref,
    _, ext_ref, partner_ref, other_ref,
):
    nb = load_ref.shape[0]
    take_edges(parity_ref[0], from_partner, from_other, ext_ref)
    tiles = (diag_ref, off_ref, prec_ref)
    edges = [lam for _, lam in sweep_blocks((0, nb - 1), cols_ref, ext_ref, load_ref, lam_ref, *tiles)]
    send_edges(parity_ref[0], *edges, partner_ref, other_ref)


def sweep_kernel(
    cols_ref, ext_ref, load_ref, lam_ref, diag_ref, off_ref, prec_ref, lam_out, ext_out
):
    blocks, tiles = range(load_ref.shape[0]), (diag_ref, off_ref, prec_ref)
    for b, lam in sweep_blocks(blocks, cols_ref, ext_ref, load_ref, lam_ref, *tiles):
        lam_out[b] = lam
        ext_out[b + 1] = lam.astype(BF16)


def last_kernel(
    scale, parity_ref, cols_ref, from_partner, from_other, load_ref, lam_ref, diag_ref, off_ref,
    prec_ref, stiff_ref, _, adj_out, grad_out, ext_ref, adj_ref, part_ref, sems,
):
    nb, m, cols = load_ref.shape
    half = cols // 2
    take_edges(parity_ref[0], from_partner, from_other, ext_ref)
    part_ref[...] = jnp.zeros_like(part_ref)
    copies = []
    tiles = (diag_ref, off_ref, prec_ref)
    for b, lam in sweep_blocks(range(nb), cols_ref, ext_ref, load_ref, lam_ref, *tiles):
        adj_ref[b] = lam.astype(BF16)
        copies.append(pltpu.make_async_copy(adj_ref.at[b], adj_out.at[b], sems.at[b]))
        copies[-1].start()
        terms = lam * stiff_ref[b]
        part_ref[b : b + 1] = jnp.sum(terms[:, :half] + terms[:, half:], axis=0, keepdims=True)
    total = jnp.sum(jnp.transpose(part_ref[...]), axis=0, keepdims=True)
    grad_out[...] = total[:, :nb] * scale
    for copy in copies:
        copy.wait()


IN_VMEM = pl.BlockSpec(memory_space=pltpu.VMEM)
IN_SMEM = pl.BlockSpec(memory_space=pltpu.SMEM)
IN_HBM = pl.BlockSpec(memory_space=pltpu.HBM)


def call(kernel, outs, ins, out_specs=None, scratch=(), aliases=None, mflops=1):
    return pl.pallas_call(
        kernel,
        out_shape=outs,
        in_specs=ins,
        out_specs=out_specs or tuple([IN_VMEM] * len(outs)),
        scratch_shapes=list(scratch),
        input_output_aliases=aliases or {},
        compiler_params=pltpu.CompilerParams(vmem_limit_bytes=VMEM_LIMIT),
        cost_estimate=pl.CostEstimate(
            flops=mflops * 1000000, bytes_accessed=4000000, transcendentals=0
        ),
    )


def swap_edges(to_partner, to_other, axis):
    count = lax.axis_size(axis)
    pairs = [(i, i ^ 1) for i in range(count)]
    others = [(i, i - 1 if i % 2 == 0 else i + 1) for i in range(1, count - 1)]
    return lax.ppermute(to_partner, axis, pairs), lax.ppermute(to_other, axis, others)


def shards(
    response, measured, sensor_owner, sensor_row, adj_diag, adj_off, block_cols, precond, stiff_deriv
):
    resp = response[0]
    diag, off, prec = adj_diag[0], adj_off[0], precond[0]
    nb, m, cols = resp.shape
    peers = lax.axis_size("sub")
    sensors = sensor_owner.shape[0]
    shape = jax.ShapeDtypeStruct
    code = (sensor_owner * 2048 + sensor_row).astype(F32).reshape(1, sensors)
    place_id = lax.axis_index("sub") & 1
    near = block_cols.reshape(-1)
    code, place_id, near = lax.optimization_barrier((code, place_id, near))
    (packed,) = call(
        functools.partial(pack_kernel, m), (shape((peers * SLOTS, cols), BF16),), [IN_VMEM] * 2
    )(code, measured[0])
    recv = lax.all_to_all(packed.reshape(peers, SLOTS, cols), "sub", 0, 0, tiled=True)
    recv = recv.reshape(peers * SLOTS, cols)
    parity = place_id.astype(jnp.int32).reshape(1)

    whole32, whole16 = shape((nb, m, cols), F32), shape((nb, m, cols), BF16)
    wide16, edge = shape((nb + 2, m, cols), BF16), shape((m, cols), BF16)
    place, to_partner, to_other = call(
        edge_kernel,
        (shape((m, peers * SLOTS), jnp.int32), edge, edge),
        [IN_SMEM] + [IN_VMEM] * 3,
    )(parity, recv, resp, prec)
    from_partner, from_other = swap_edges(to_partner, to_other, "sub")
    load, lam, ext, stiff_resp = call(
        load_kernel, (whole32, whole32, wide16, whole32), [IN_VMEM] * 5, mflops=2000
    )(place, recv, resp, prec, stiff_deriv)

    ext, to_partner, to_other = call(
        sweep_edge_kernel,
        (wide16, edge, edge),
        [IN_SMEM] * 2 + [IN_VMEM] * 8,
        aliases={9: 0},
    )(parity, near, from_partner, from_other, load, lam, diag, off, prec, ext)
    from_partner, from_other = swap_edges(to_partner, to_other, "sub")
    lam, ext = call(sweep_kernel, (whole32, wide16), [IN_SMEM] + [IN_VMEM] * 6, mflops=2000)(
        near, ext, load, lam, diag, off, prec
    )

    scale = 1.0 / math.sqrt(m * cols)
    adjoint, grad, _ = call(
        functools.partial(last_kernel, scale),
        (whole16, shape((1, nb), F32), wide16),
        [IN_SMEM] * 2 + [IN_VMEM] * 9,
        out_specs=(IN_HBM, IN_VMEM, IN_VMEM),
        scratch=[
            pltpu.VMEM((nb, m, cols), BF16),
            pltpu.VMEM((128, 128), F32),
            pltpu.SemaphoreType.DMA((nb,)),
        ],
        aliases={10: 2},
    )(parity, near, from_partner, from_other, load, lam, diag, off, prec, stiff_resp, ext)
    gradient = lax.psum(grad.reshape(nb), "freq")
    return (adjoint[None], gradient)


def solution(mesh):
    in_specs = (
        P("freq", "sub", None, None),
        P("freq", "sub", None),
        P("sub"),
        P("sub"),
        P("freq", "sub", None, None, None),
        P("freq", "sub", None, None, None, None),
        P("sub", None),
        P("freq", "sub", None, None, None),
        P("sub", None, None),
    )
    out_specs = (P("freq", "sub", None, None), P("sub"))
    return jax.shard_map(shards, mesh=mesh, in_specs=in_specs, out_specs=out_specs, check_vma=False)
```

```python
import functools
import math

import jax
import jax.numpy as jnp
from jax import lax
from jax.experimental import pallas as pl
from jax.experimental.pallas import tpu as pltpu
from jax.sharding import PartitionSpec as P

SLOTS = 4
VMEM_LIMIT = 16 * 1024 * 1024

F32 = jnp.float32
BF16 = jnp.bfloat16


def iota(shape, dim):
    return lax.broadcasted_iota(jnp.int32, shape, dim)


def split_product(both):
    m, half = both.shape[0] // 2, both.shape[1] // 2
    real_part = both[:m, :half] - both[m:, half:]
    imag_part = both[:m, half:] + both[m:, :half]
    return jnp.concatenate([real_part, imag_part], axis=1)


def stacked(tile_pair):
    return tile_pair.reshape(tile_pair.shape[0] * tile_pair.shape[1], tile_pair.shape[2])


def complex_product(tile_pair, block):
    return split_product(jnp.dot(stacked(tile_pair), block, preferred_element_type=F32))


def pack_kernel(rows_per, code_ref, measured_ref, out_ref):
    count = measured_ref.shape[0]
    slots_all = out_ref.shape[0]
    code = code_ref[...]
    owner = code.astype(jnp.int32) >> 11
    lanes = jnp.broadcast_to(jnp.pad(code, ((0, 0), (0, 128 - count))), (128, 128))
    code_col = jnp.transpose(lanes)[:count, :count].astype(jnp.int32)
    owner_col = code_col >> 11
    row_col = code_col & 2047
    same = jnp.broadcast_to(owner, (count, count)) == owner_col
    sub = iota((count, count), 0)
    lane = iota((count, count), 1)
    rank_row = jnp.sum(jnp.where(same & (sub < lane), 1, 0), axis=0, keepdims=True)
    rank_col = jnp.sum(jnp.where(same & (lane < sub), 1, 0), axis=1, keepdims=True)
    place = iota((slots_all, count), 0)
    here = (place >> 2) == owner
    slot = place & 3
    pick = jnp.where(here & (slot == rank_row), 1.0, 0.0).astype(BF16)
    tell = jnp.where(here & (slot == SLOTS - 1), 1.0, 0.0).astype(BF16)
    width = iota((count, 128), 1)
    row_wide = jnp.broadcast_to(row_col[:, :1], (count, 128))
    block = row_wide // rows_per
    inner = row_wide - block * rows_per
    numbers = jnp.where(width == rank_col, block + 1, 0) + jnp.where(
        width == rank_col + SLOTS, inner, 0
    )
    numbers = numbers.astype(F32).astype(BF16)
    rows = jnp.dot(pick, measured_ref[...], preferred_element_type=F32)
    told = jnp.dot(tell, numbers, preferred_element_type=F32)
    half = rows.shape[-1] // 2
    out_ref[:, :half] = (rows[:, :half] + told).astype(BF16)
    out_ref[:, half:] = rows[:, half:].astype(BF16)


def send_edges(parity, first, last, other_ref, partner_ref):
    even = parity == 0
    partner_ref[...] = jnp.where(even, last, first).astype(BF16)
    other_ref[...] = jnp.where(even, first, last).astype(BF16)


def take_edges(parity, other_ref, partner_ref, ext_ref):
    top = ext_ref.shape[0] - 1
    even = parity == 0
    ext_ref[jnp.where(even, top, 0)] = partner_ref[...]
    ext_ref[jnp.where(even, 0, top)] = other_ref[...]


def make_load(first, count, place_ref, recv, ones, resp_ref):
    m = place_ref.shape[0]
    half = recv.shape[1] // 2
    place = place_ref[...]
    hit = jnp.concatenate(
        [jnp.where(place == (first + i) * m, 1.0, 0.0).astype(BF16) for i in range(count)], axis=0
    )
    summed = jnp.dot(hit, recv, preferred_element_type=F32)
    number = jnp.dot(hit, ones, preferred_element_type=F32)
    loads = []
    for i in range(count):
        rows = slice(i * m, (i + 1) * m)
        resp = resp_ref[first + i].astype(F32)
        loads.append(
            jnp.concatenate([number[rows], number[rows]], axis=1) * resp - summed[rows]
        )
    return loads


def edge_kernel(parity_ref, recv_ref, resp_ref, prec_ref, place_ref, other_ref, partner_ref):
    nb, m, cols = resp_ref.shape
    half = cols // 2
    places = recv_ref.shape[0]
    recv = recv_ref[...]
    turned = jnp.transpose(recv[:, :half].astype(F32)).astype(BF16)
    lane = iota((m, half), 1)
    slot = iota((m, places), 1) & 3
    where_row = jnp.full((m, places), -1.0, F32)
    for s in range(SLOTS - 1):
        weights = jnp.where(lane == s, m, 0) + jnp.where(lane == s + SLOTS, 1, 0)
        told = jnp.dot(weights.astype(F32).astype(BF16), turned, preferred_element_type=F32)
        told = pltpu.roll(told, places + s - (SLOTS - 1), 1)
        where_row = jnp.where(slot == s, told - m, where_row)
    place_ref[...] = where_row.astype(jnp.int32) - iota((m, places), 0)
    ones = jnp.ones((places, half), BF16)
    edges = []
    for b in (0, nb - 1):
        load = make_load(b, 1, place_ref, recv, ones, resp_ref)[0]
        edges.append(complex_product(prec_ref[b], load.astype(BF16)))
    send_edges(parity_ref[0], *edges, other_ref, partner_ref)


def load_kernel(
    place_ref, recv_ref, resp_ref, prec_ref, stiff_ref, load_ref, lam_ref, ext_ref, stiff_out
):
    nb, m, cols = resp_ref.shape
    recv = recv_ref[...]
    ones = jnp.ones((recv.shape[0], cols // 2), BF16)
    group = 4 if nb % 4 == 0 else 1
    for first in range(0, nb, group):
        loads = make_load(first, group, place_ref, recv, ones, resp_ref)
        for i, load in enumerate(loads):
            b = first + i
            load_ref[b] = load
            lam = complex_product(prec_ref[b], load.astype(BF16))
            lam_ref[b] = lam
            ext_ref[b + 1] = lam.astype(BF16)
    for b in range(nb):
        stiff_out[b] = jnp.dot(stiff_ref[b], resp_ref[b], preferred_element_type=F32)


def sweep_blocks(blocks, cols_ref, ext_ref, load_ref, lam_ref, diag_ref, off_ref, prec_ref):
    near = off_ref.shape[1]
    updates = []
    for b in blocks:
        tiles = [stacked(diag_ref[b])] + [stacked(off_ref[b, k]) for k in range(near)]
        parts = [ext_ref[b + 1]] + [ext_ref[cols_ref[k, b]] for k in range(near)]
        both = None
        for i in range(0, near + 1, 2):
            part = jnp.dot(
                jnp.concatenate(tiles[i : i + 2], axis=1),
                jnp.concatenate(parts[i : i + 2], axis=0),
                preferred_element_type=F32,
            )
            both = part if both is None else both + part
        updates.append((load_ref[b] - split_product(both)).astype(BF16))
    for b, update in zip(blocks, updates):
        yield b, lam_ref[b] + complex_product(prec_ref[b], update)


def sweep_edge_kernel(
    parity_ref, cols_ref, from_other, from_partner, load_ref, lam_ref, diag_ref, off_ref, prec_ref,
    _, ext_ref, other_ref, partner_ref,
):
    nb = load_ref.shape[0]
    take_edges(parity_ref[0], from_other, from_partner, ext_ref)
    tiles = (diag_ref, off_ref, prec_ref)
    edges = [lam for _, lam in sweep_blocks((0, nb - 1), cols_ref, ext_ref, load_ref, lam_ref, *tiles)]
    send_edges(parity_ref[0], *edges, other_ref, partner_ref)


def sweep_kernel(
    cols_ref, ext_ref, load_ref, lam_ref, diag_ref, off_ref, prec_ref, lam_out, ext_out
):
    blocks, tiles = range(load_ref.shape[0]), (diag_ref, off_ref, prec_ref)
    for b, lam in sweep_blocks(blocks, cols_ref, ext_ref, load_ref, lam_ref, *tiles):
        lam_out[b] = lam
        ext_out[b + 1] = lam.astype(BF16)


def last_kernel(
    scale, parity_ref, cols_ref, from_other, from_partner, load_ref, lam_ref, diag_ref, off_ref,
    prec_ref, stiff_ref, _, adj_out, grad_out, ext_ref, adj_ref, part_ref, sems,
):
    nb, m, cols = load_ref.shape
    half = cols // 2
    take_edges(parity_ref[0], from_other, from_partner, ext_ref)
    part_ref[...] = jnp.zeros_like(part_ref)
    copies = []
    tiles = (diag_ref, off_ref, prec_ref)
    for b, lam in sweep_blocks(range(nb), cols_ref, ext_ref, load_ref, lam_ref, *tiles):
        adj_ref[b] = lam.astype(BF16)
        copies.append(pltpu.make_async_copy(adj_ref.at[b], adj_out.at[b], sems.at[b]))
        copies[-1].start()
        terms = lam * stiff_ref[b]
        part_ref[b : b + 1] = jnp.sum(terms[:, :half] + terms[:, half:], axis=0, keepdims=True)
    total = jnp.sum(jnp.transpose(part_ref[...]), axis=0, keepdims=True)
    grad_out[...] = total[:, :nb] * scale
    for copy in copies:
        copy.wait()


IN_VMEM = pl.BlockSpec(memory_space=pltpu.VMEM)
IN_SMEM = pl.BlockSpec(memory_space=pltpu.SMEM)
IN_HBM = pl.BlockSpec(memory_space=pltpu.HBM)


def call(kernel, outs, ins, out_specs=None, scratch=(), aliases=None, mflops=1):
    return pl.pallas_call(
        kernel,
        out_shape=outs,
        in_specs=ins,
        out_specs=out_specs or tuple([IN_VMEM] * len(outs)),
        scratch_shapes=list(scratch),
        input_output_aliases=aliases or {},
        compiler_params=pltpu.CompilerParams(vmem_limit_bytes=VMEM_LIMIT),
        cost_estimate=pl.CostEstimate(
            flops=mflops * 1000000, bytes_accessed=4000000, transcendentals=0
        ),
    )


def swap_edges(to_other, to_partner, axis):
    count = lax.axis_size(axis)
    pairs = [(i, i ^ 1) for i in range(count)]
    others = [(i, i - 1 if i % 2 == 0 else i + 1) for i in range(1, count - 1)]
    return lax.ppermute(to_other, axis, others), lax.ppermute(to_partner, axis, pairs)


def shards(
    response, measured, sensor_owner, sensor_row, adj_diag, adj_off, block_cols, precond, stiff_deriv
):
    resp = response[0]
    diag, off, prec = adj_diag[0], adj_off[0], precond[0]
    nb, m, cols = resp.shape
    peers = lax.axis_size("sub")
    sensors = sensor_owner.shape[0]
    shape = jax.ShapeDtypeStruct
    code = (sensor_owner * 2048 + sensor_row).astype(F32).reshape(1, sensors)
    place_id = lax.axis_index("sub") & 1
    near = block_cols.T
    code, place_id = lax.optimization_barrier((code, place_id))
    (packed,) = call(
        functools.partial(pack_kernel, m), (shape((peers * SLOTS, cols), BF16),), [IN_VMEM] * 2
    )(code, measured[0])
    recv = lax.all_to_all(packed.reshape(peers, SLOTS, cols), "sub", 0, 0, tiled=True)
    recv = recv.reshape(peers * SLOTS, cols)
    parity = place_id.astype(jnp.int32).reshape(1)

    whole32, whole16 = shape((nb, m, cols), F32), shape((nb, m, cols), BF16)
    wide16, edge = shape((nb + 2, m, cols), BF16), shape((m, cols), BF16)
    place, to_other, to_partner = call(
        edge_kernel,
        (shape((m, peers * SLOTS), jnp.int32), edge, edge),
        [IN_SMEM] + [IN_VMEM] * 3,
    )(parity, recv, resp, prec)
    from_other, from_partner = swap_edges(to_other, to_partner, "sub")
    load, lam, ext, stiff_resp = call(
        load_kernel, (whole32, whole32, wide16, whole32), [IN_VMEM] * 5, mflops=2000
    )(place, recv, resp, prec, stiff_deriv)

    ext, to_other, to_partner = call(
        sweep_edge_kernel,
        (wide16, edge, edge),
        [IN_SMEM] * 2 + [IN_VMEM] * 8,
        aliases={9: 0},
    )(parity, near, from_other, from_partner, load, lam, diag, off, prec, ext)
    from_other, from_partner = swap_edges(to_other, to_partner, "sub")
    lam, ext = call(sweep_kernel, (whole32, wide16), [IN_SMEM] + [IN_VMEM] * 6, mflops=2000)(
        near, ext, load, lam, diag, off, prec
    )

    scale = 1.0 / math.sqrt(m * cols)
    adjoint, grad, _ = call(
        functools.partial(last_kernel, scale),
        (whole16, shape((1, nb), F32), wide16),
        [IN_SMEM] * 2 + [IN_VMEM] * 9,
        out_specs=(IN_HBM, IN_VMEM, IN_VMEM),
        scratch=[
            pltpu.VMEM((nb, m, cols), BF16),
            pltpu.VMEM((128, 128), F32),
            pltpu.SemaphoreType.DMA((nb,)),
        ],
        aliases={10: 2},
    )(parity, near, from_other, from_partner, load, lam, diag, off, prec, stiff_resp, ext)
    gradient = lax.psum(grad.reshape(nb), "freq")
    return (adjoint[None], gradient)


def solution(mesh):
    in_specs = (
        P("freq", "sub", None, None),
        P("freq", "sub", None),
        P("sub"),
        P("sub"),
        P("freq", "sub", None, None, None),
        P("freq", "sub", None, None, None, None),
        P("sub", None),
        P("freq", "sub", None, None, None),
        P("sub", None, None),
    )
    out_specs = (P("freq", "sub", None, None), P("sub"))
    return jax.shard_map(shards, mesh=mesh, in_specs=in_specs, out_specs=out_specs, check_vma=False)
```

```python
import functools
import math

import jax
import jax.numpy as jnp
from jax import lax
from jax.experimental import pallas as pl
from jax.experimental.pallas import tpu as pltpu
from jax.sharding import PartitionSpec as P

SLOTS = 3
CODE = 2048
VMEM_LIMIT = 16 * 1024 * 1024

F32 = jnp.float32
BF16 = jnp.bfloat16


def iota(shape, dim):
    return lax.broadcasted_iota(jnp.int32, shape, dim)


def split_product(both):
    m, half = both.shape[0] // 2, both.shape[1] // 2
    real_part = both[:m, :half] - both[m:, half:]
    imag_part = both[:m, half:] + both[m:, :half]
    return jnp.concatenate([real_part, imag_part], axis=1)


def stacked(tile_pair):
    return tile_pair.reshape(tile_pair.shape[0] * tile_pair.shape[1], tile_pair.shape[2])


def complex_product(tile_pair, block):
    return split_product(jnp.dot(stacked(tile_pair), block, preferred_element_type=F32))


def pack_kernel(
    rows_per, owner_hbm, row_hbm, measured_hbm, out_ref, owner_ref, row_ref, measured_ref, sems
):
    copies = [
        pltpu.make_async_copy(source, target, sems.at[i])
        for i, (source, target) in enumerate(
            ((owner_hbm, owner_ref), (row_hbm, row_ref), (measured_hbm, measured_ref))
        )
    ]
    for copy in copies:
        copy.start()
    for copy in copies[:2]:
        copy.wait()
    count = measured_ref.shape[0]
    owner = owner_ref[...]
    code = (owner * CODE + row_ref[...]).astype(F32)
    lanes = jnp.broadcast_to(jnp.pad(code, ((0, 0), (0, 128 - count))), (128, 128))
    code_col = jnp.transpose(lanes)[:count].astype(jnp.int32)
    owner_col = code_col[:, :count] // CODE
    row_wide = code_col & (CODE - 1)
    same = jnp.broadcast_to(owner, (count, count)) == owner_col
    sub = iota((count, count), 0)
    lane = iota((count, count), 1)
    rank_row = jnp.sum(jnp.where(same & (sub < lane), 1, 0), axis=0, keepdims=True)
    rank_col = jnp.sum(jnp.where(same & (lane < sub), 1, 0), axis=1, keepdims=True)
    width = iota((count, 128), 1)
    block = row_wide // rows_per
    inner = row_wide - block * rows_per
    numbers = jnp.where(width == rank_col, block + 1, 0)
    numbers += jnp.where(width == rank_col + SLOTS, inner, 0)
    numbers = numbers.astype(F32).astype(BF16)
    place = iota((out_ref.shape[0], count), 0)
    here = (place >> 1) == owner
    first_half = (place & 1) == 0
    copies[2].wait()
    tell = jnp.where(here & first_half, 1.0, 0.0).astype(BF16)
    told = jnp.dot(tell, numbers, preferred_element_type=F32)
    out_ref[:, SLOTS * 128 :] = told.astype(BF16)
    low, high = measured_ref[:, :128], measured_ref[:, 128:]
    for s in range(SLOTS):
        mine = here & (rank_row == s)
        pick_low = jnp.where(mine & first_half, 1.0, 0.0).astype(BF16)
        pick_high = jnp.where(mine & ~first_half, 1.0, 0.0).astype(BF16)
        out_ref[:, s * 128 : (s + 1) * 128] = (
            jnp.dot(pick_low, low, preferred_element_type=F32)
            + jnp.dot(pick_high, high, preferred_element_type=F32)
        ).astype(BF16)


def send_edges(parity, first, last, other_ref, partner_ref):
    even = parity == 0
    partner_ref[...] = jnp.where(even, last, first).astype(BF16)
    other_ref[...] = jnp.where(even, first, last).astype(BF16)


def take_edges(parity, other_ref, partner_ref, ext_ref):
    top = ext_ref.shape[0] - 1
    even = parity == 0
    ext_ref[jnp.where(even, top, 0)] = partner_ref[...]
    ext_ref[jnp.where(even, 0, top)] = other_ref[...]


def make_load(first, count, place_ref, recv, ones, resp_ref):
    m = place_ref.shape[0]
    half = recv.shape[1] // 2
    place = place_ref[...]
    hit = jnp.concatenate(
        [jnp.where(place == (first + i) * m, 1.0, 0.0).astype(BF16) for i in range(count)], axis=0
    )
    summed = jnp.dot(hit, recv, preferred_element_type=F32)
    number = jnp.dot(hit, ones, preferred_element_type=F32)
    loads = []
    for i in range(count):
        rows = slice(i * m, (i + 1) * m)
        resp = resp_ref[first + i].astype(F32)
        loads.append(
            jnp.concatenate([number[rows], number[rows]], axis=1) * resp - summed[rows]
        )
    return loads


def unpack(recv_ref, place_ref, rows_ref, line_ref):
    peers, width = recv_ref.shape[0] // 2, recv_ref.shape[1] // (SLOTS + 1)
    m = place_ref.shape[0]
    line_ref[...] = recv_ref[:, SLOTS * width :].astype(F32)
    numbers = jnp.transpose(line_ref[pl.ds(0, peers, stride=2), :]).astype(BF16)
    lane = iota((m, width), 1)
    for s in range(SLOTS):
        weights = jnp.where(lane == s, m, 0) + jnp.where(lane == s + SLOTS, 1, 0)
        told = jnp.dot(weights.astype(F32).astype(BF16), numbers, preferred_element_type=F32)
        place_ref[:, s * peers : (s + 1) * peers] = (
            told.astype(jnp.int32) - m - iota((m, peers), 0)
        )
        line_ref[...] = recv_ref[:, s * width : (s + 1) * width].astype(F32)
        for i in range(2):
            rows_ref[s * peers : (s + 1) * peers, i * width : (i + 1) * width] = line_ref[
                pl.ds(i, peers, stride=2), :
            ].astype(BF16)


def edge_kernel(
    parity_ref, recv_ref, resp_ref, prec_ref, place_ref, rows_ref, other_ref, partner_ref,
    line_ref,
):
    nb, m, cols = resp_ref.shape
    half = cols // 2
    unpack(recv_ref, place_ref, rows_ref, line_ref)
    recv = rows_ref[...]
    places = recv.shape[0]
    ones = jnp.ones((places, half), BF16)
    edges = []
    for b in (0, nb - 1):
        load = make_load(b, 1, place_ref, recv, ones, resp_ref)[0]
        edges.append(complex_product(prec_ref[b], load.astype(BF16)))
    send_edges(parity_ref[0], *edges, other_ref, partner_ref)


def load_kernel(
    place_ref, recv_ref, resp_ref, prec_ref, stiff_ref, load_ref, lam_ref, ext_ref, stiff_out
):
    nb, m, cols = resp_ref.shape
    recv = recv_ref[...]
    ones = jnp.ones((recv.shape[0], cols // 2), BF16)
    group = 4 if nb % 4 == 0 else 1
    for first in range(0, nb, group):
        loads = make_load(first, group, place_ref, recv, ones, resp_ref)
        for i, load in enumerate(loads):
            b = first + i
            load_ref[b] = load
            lam = complex_product(prec_ref[b], load.astype(BF16))
            lam_ref[b] = lam
            ext_ref[b + 1] = lam.astype(BF16)
    for b in range(nb):
        stiff_out[b] = jnp.dot(stiff_ref[b], resp_ref[b], preferred_element_type=F32)


def sweep_blocks(blocks, cols_ref, ext_ref, load_ref, lam_ref, diag_ref, off_ref, prec_ref):
    near = off_ref.shape[1]
    updates = []
    for b in blocks:
        tiles = [stacked(diag_ref[b])] + [stacked(off_ref[b, k]) for k in range(near)]
        parts = [ext_ref[b + 1]] + [ext_ref[cols_ref[k, b]] for k in range(near)]
        both = None
        for i in range(0, near + 1, 2):
            part = jnp.dot(
                jnp.concatenate(tiles[i : i + 2], axis=1),
                jnp.concatenate(parts[i : i + 2], axis=0),
                preferred_element_type=F32,
            )
            both = part if both is None else both + part
        updates.append((load_ref[b] - split_product(both)).astype(BF16))
    for b, update in zip(blocks, updates):
        yield b, lam_ref[b] + complex_product(prec_ref[b], update)


def sweep_edge_kernel(
    parity_ref, cols_ref, from_other, from_partner, load_ref, lam_ref, diag_ref, off_ref, prec_ref,
    _, ext_ref, other_ref, partner_ref,
):
    nb = load_ref.shape[0]
    take_edges(parity_ref[0], from_other, from_partner, ext_ref)
    tiles = (diag_ref, off_ref, prec_ref)
    edges = [lam for _, lam in sweep_blocks((0, nb - 1), cols_ref, ext_ref, load_ref, lam_ref, *tiles)]
    send_edges(parity_ref[0], *edges, other_ref, partner_ref)


def sweep_kernel(
    cols_ref, ext_ref, load_ref, lam_ref, diag_ref, off_ref, prec_ref, lam_out, ext_out
):
    blocks, tiles = range(load_ref.shape[0]), (diag_ref, off_ref, prec_ref)
    for b, lam in sweep_blocks(blocks, cols_ref, ext_ref, load_ref, lam_ref, *tiles):
        lam_out[b] = lam
        ext_out[b + 1] = lam.astype(BF16)


def last_kernel(
    scale, parity_ref, cols_ref, from_other, from_partner, load_ref, lam_ref, diag_ref, off_ref,
    prec_ref, stiff_ref, _, adj_out, grad_out, ext_ref, part_ref,
):
    nb, m, cols = load_ref.shape
    half = cols // 2
    take_edges(parity_ref[0], from_other, from_partner, ext_ref)
    part_ref[...] = jnp.zeros_like(part_ref)
    tiles = (diag_ref, off_ref, prec_ref)
    for b, lam in sweep_blocks(range(nb), cols_ref, ext_ref, load_ref, lam_ref, *tiles):
        adj_out[b] = lam.astype(BF16)
        terms = lam * stiff_ref[b]
        part_ref[b : b + 1] = jnp.sum(terms[:, :half] + terms[:, half:], axis=0, keepdims=True)
    total = jnp.sum(jnp.transpose(part_ref[...]), axis=0, keepdims=True)
    grad_out[...] = total[:, :nb] * scale


IN_VMEM = pl.BlockSpec(memory_space=pltpu.VMEM)
IN_SMEM = pl.BlockSpec(memory_space=pltpu.SMEM)


def call(kernel, outs, ins, out_specs=None, scratch=(), aliases=None, mflops=1):
    return pl.pallas_call(
        kernel,
        out_shape=outs,
        in_specs=ins,
        out_specs=out_specs or tuple([IN_VMEM] * len(outs)),
        scratch_shapes=list(scratch),
        input_output_aliases=aliases or {},
        compiler_params=pltpu.CompilerParams(vmem_limit_bytes=VMEM_LIMIT),
        cost_estimate=pl.CostEstimate(
            flops=mflops * 1000000, bytes_accessed=4000000, transcendentals=0
        ),
    )


def swap_edges(to_other, to_partner, axis):
    count = lax.axis_size(axis)
    pairs = [(i, i ^ 1) for i in range(count)]
    others = [(i, i - 1 if i % 2 == 0 else i + 1) for i in range(1, count - 1)]
    return lax.ppermute(to_other, axis, others), lax.ppermute(to_partner, axis, pairs)


def shards(
    response, measured, sensor_owner, sensor_row, adj_diag, adj_off, block_cols, precond, stiff_deriv
):
    resp = response[0]
    diag, off, prec = adj_diag[0], adj_off[0], precond[0]
    nb, m, cols = resp.shape
    peers = lax.axis_size("sub")
    sensors = sensor_owner.shape[0]
    shape = jax.ShapeDtypeStruct
    owner, row = sensor_owner.reshape(1, sensors), sensor_row.reshape(1, sensors)
    owner, row, rows_in, place_id = lax.optimization_barrier(
        (owner, row, measured[0], lax.axis_index("sub") & 1)
    )
    near = block_cols.T
    numbers = pltpu.VMEM((1, sensors), jnp.int32)
    (packed,) = call(
        functools.partial(pack_kernel, m),
        (shape((2 * peers, (SLOTS + 1) * cols // 2), BF16),),
        [pl.BlockSpec(memory_space=pltpu.HBM)] * 3,
        scratch=[numbers, numbers, pltpu.VMEM((sensors, cols), BF16), pltpu.SemaphoreType.DMA((3,))],
    )(*(pltpu.with_memory_space_constraint(x, pltpu.HBM) for x in (owner, row, rows_in)))
    recv = lax.all_to_all(
        packed.reshape(peers, 2, -1), "sub", 0, 0, tiled=True
    ).reshape(packed.shape)
    parity = place_id.astype(jnp.int32).reshape(1)

    whole32, whole16 = shape((nb, m, cols), F32), shape((nb, m, cols), BF16)
    wide16, edge = shape((nb + 2, m, cols), BF16), shape((m, cols), BF16)
    place, rows, to_other, to_partner = call(
        edge_kernel,
        (shape((m, peers * SLOTS), jnp.int32), shape((peers * SLOTS, cols), BF16), edge, edge),
        [IN_SMEM] + [IN_VMEM] * 3,
        scratch=[pltpu.VMEM((2 * peers, cols // 2), F32)],
    )(parity, recv, resp, prec)
    from_other, from_partner = swap_edges(to_other, to_partner, "sub")
    load, lam, ext, stiff_resp = call(
        load_kernel, (whole32, whole32, wide16, whole32), [IN_VMEM] * 5, mflops=2000
    )(place, rows, resp, prec, stiff_deriv)

    ext, to_other, to_partner = call(
        sweep_edge_kernel,
        (wide16, edge, edge),
        [IN_SMEM] * 2 + [IN_VMEM] * 8,
        aliases={9: 0},
    )(parity, near, from_other, from_partner, load, lam, diag, off, prec, ext)
    from_other, from_partner = swap_edges(to_other, to_partner, "sub")
    lam, ext = call(sweep_kernel, (whole32, wide16), [IN_SMEM] + [IN_VMEM] * 6, mflops=2000)(
        near, ext, load, lam, diag, off, prec
    )

    scale = 1.0 / math.sqrt(m * cols)
    adjoint, grad, _ = call(
        functools.partial(last_kernel, scale),
        (whole16, shape((1, nb), F32), wide16),
        [IN_SMEM] * 2 + [IN_VMEM] * 9,
        scratch=[pltpu.VMEM((128, 128), F32)],
        aliases={10: 2},
    )(parity, near, from_other, from_partner, load, lam, diag, off, prec, stiff_resp, ext)
    gradient = lax.psum(grad.reshape(nb), "freq")
    return (adjoint[None], gradient)


def solution(mesh):
    in_specs = (
        P("freq", "sub", None, None),
        P("freq", "sub", None),
        P("sub"),
        P("sub"),
        P("freq", "sub", None, None, None),
        P("freq", "sub", None, None, None, None),
        P("sub", None),
        P("freq", "sub", None, None, None),
        P("sub", None, None),
    )
    out_specs = (P("freq", "sub", None, None), P("sub"))
    return jax.shard_map(shards, mesh=mesh, in_specs=in_specs, out_specs=out_specs, check_vma=False)
```

```python
import functools
import math

import jax
import jax.numpy as jnp
from jax import lax
from jax.experimental import pallas as pl
from jax.experimental.pallas import tpu as pltpu
from jax.sharding import PartitionSpec as P

SLOTS = 3
CODE = 2048
VMEM_LIMIT = 16 * 1024 * 1024

F32 = jnp.float32
BF16 = jnp.bfloat16


def iota(shape, dim):
    return lax.broadcasted_iota(jnp.int32, shape, dim)


def split_product(both):
    m, half = both.shape[0] // 2, both.shape[1] // 2
    real_part = both[:m, :half] - both[m:, half:]
    imag_part = both[:m, half:] + both[m:, :half]
    return jnp.concatenate([real_part, imag_part], axis=1)


def stacked(tile_pair):
    return tile_pair.reshape(tile_pair.shape[0] * tile_pair.shape[1], tile_pair.shape[2])


def complex_product(tile_pair, block):
    return split_product(jnp.dot(stacked(tile_pair), block, preferred_element_type=F32))


def pack_kernel(
    rows_per, owner_hbm, row_hbm, measured_hbm, out_ref, owner_ref, row_ref, measured_ref, sems
):
    copies = [
        pltpu.make_async_copy(source, target, sems.at[i])
        for i, (source, target) in enumerate(
            ((owner_hbm, owner_ref), (row_hbm, row_ref), (measured_hbm, measured_ref))
        )
    ]
    for copy in copies:
        copy.start()
    for copy in copies[:2]:
        copy.wait()
    count = measured_ref.shape[0]
    owner = owner_ref[...]
    code = (owner * CODE + row_ref[...]).astype(F32)
    lanes = jnp.broadcast_to(jnp.pad(code, ((0, 0), (0, 128 - count))), (128, 128))
    code_col = jnp.transpose(lanes)[:count].astype(jnp.int32)
    owner_col = code_col[:, :count] // CODE
    row_wide = code_col & (CODE - 1)
    same = jnp.broadcast_to(owner, (count, count)) == owner_col
    sub = iota((count, count), 0)
    lane = iota((count, count), 1)
    rank_row = jnp.sum(jnp.where(same & (sub < lane), 1, 0), axis=0, keepdims=True)
    rank_col = jnp.sum(jnp.where(same & (lane < sub), 1, 0), axis=1, keepdims=True)
    width = iota((count, 128), 1)
    block = row_wide // rows_per
    inner = row_wide - block * rows_per
    numbers = jnp.where(width == rank_col, block + 1, 0)
    numbers += jnp.where(width == rank_col + SLOTS, inner, 0)
    numbers = numbers.astype(F32).astype(BF16)
    place = iota((out_ref.shape[0], count), 0)
    here = (place >> 1) == owner
    first_half = (place & 1) == 0
    copies[2].wait()
    tell = jnp.where(here & first_half, 1.0, 0.0).astype(BF16)
    told = jnp.dot(tell, numbers, preferred_element_type=F32)
    out_ref[:, SLOTS * 128 :] = told.astype(BF16)
    low, high = measured_ref[:, :128], measured_ref[:, 128:]
    for s in range(SLOTS):
        mine = here & (rank_row == s)
        pick_low = jnp.where(mine & first_half, 1.0, 0.0).astype(BF16)
        pick_high = jnp.where(mine & ~first_half, 1.0, 0.0).astype(BF16)
        out_ref[:, s * 128 : (s + 1) * 128] = (
            jnp.dot(pick_low, low, preferred_element_type=F32)
            + jnp.dot(pick_high, high, preferred_element_type=F32)
        ).astype(BF16)


def send_edges(parity, first, last, other_ref, partner_ref):
    even = parity == 0
    partner_ref[...] = jnp.where(even, last, first).astype(BF16)
    other_ref[...] = jnp.where(even, first, last).astype(BF16)


def take_edges(parity, other_ref, partner_ref, ext_ref):
    top = ext_ref.shape[0] - 1
    even = parity == 0
    ext_ref[jnp.where(even, top, 0)] = partner_ref[...]
    ext_ref[jnp.where(even, 0, top)] = other_ref[...]


def make_load(first, count, place_ref, recv, ones, resp_ref):
    m = place_ref.shape[0]
    half = recv.shape[1] // 2
    place = place_ref[...]
    hit = jnp.concatenate(
        [jnp.where(place == (first + i) * m, 1.0, 0.0).astype(BF16) for i in range(count)], axis=0
    )
    summed = jnp.dot(hit, recv, preferred_element_type=F32)
    number = jnp.dot(hit, ones, preferred_element_type=F32)
    loads = []
    for i in range(count):
        rows = slice(i * m, (i + 1) * m)
        resp = resp_ref[first + i].astype(F32)
        loads.append(
            jnp.concatenate([number[rows], number[rows]], axis=1) * resp - summed[rows]
        )
    return loads


def unpack(recv_ref, place_ref, rows_ref, line_ref):
    peers, width = recv_ref.shape[0] // 2, recv_ref.shape[1] // (SLOTS + 1)
    m = place_ref.shape[0]
    line_ref[...] = recv_ref[:, SLOTS * width :].astype(F32)
    numbers = jnp.transpose(line_ref[pl.ds(0, peers, stride=2), :]).astype(BF16)
    lane = iota((m, width), 1)
    for s in range(SLOTS):
        weights = jnp.where(lane == s, m, 0) + jnp.where(lane == s + SLOTS, 1, 0)
        told = jnp.dot(weights.astype(F32).astype(BF16), numbers, preferred_element_type=F32)
        place_ref[:, s * peers : (s + 1) * peers] = (
            told.astype(jnp.int32) - m - iota((m, peers), 0)
        )
        line_ref[...] = recv_ref[:, s * width : (s + 1) * width].astype(F32)
        for i in range(2):
            rows_ref[s * peers : (s + 1) * peers, i * width : (i + 1) * width] = line_ref[
                pl.ds(i, peers, stride=2), :
            ].astype(BF16)


def edge_kernel(
    parity_ref, recv_ref, resp_ref, prec_ref, place_ref, rows_ref, other_ref, partner_ref,
    line_ref,
):
    nb, m, cols = resp_ref.shape
    half = cols // 2
    unpack(recv_ref, place_ref, rows_ref, line_ref)
    recv = rows_ref[...]
    places = recv.shape[0]
    ones = jnp.ones((places, half), BF16)
    edges = []
    for b in (0, nb - 1):
        load = make_load(b, 1, place_ref, recv, ones, resp_ref)[0]
        edges.append(complex_product(prec_ref[b], load.astype(BF16)))
    send_edges(parity_ref[0], *edges, other_ref, partner_ref)


def load_kernel(
    place_ref, recv_ref, resp_ref, prec_ref, stiff_ref, load_ref, lam_ref, ext_ref, stiff_out
):
    nb, m, cols = resp_ref.shape
    recv = recv_ref[...]
    ones = jnp.ones((recv.shape[0], cols // 2), BF16)
    group = 4 if nb % 4 == 0 else 1
    for first in range(0, nb, group):
        loads = make_load(first, group, place_ref, recv, ones, resp_ref)
        for i, load in enumerate(loads):
            b = first + i
            load_ref[b] = load
            lam = complex_product(prec_ref[b], load.astype(BF16))
            lam_ref[b] = lam
            ext_ref[b + 1] = lam.astype(BF16)
    for b in range(nb):
        stiff_out[b] = jnp.dot(stiff_ref[b], resp_ref[b], preferred_element_type=F32)


def sweep_blocks(blocks, cols_ref, ext_ref, load_ref, lam_ref, diag_ref, off_ref, prec_ref):
    near = off_ref.shape[1]
    updates = []
    for b in blocks:
        tiles = [stacked(diag_ref[b])] + [stacked(off_ref[b, k]) for k in range(near)]
        parts = [ext_ref[b + 1]] + [ext_ref[cols_ref[k, b]] for k in range(near)]
        both = None
        for i in range(0, near + 1, 2):
            part = jnp.dot(
                jnp.concatenate(tiles[i : i + 2], axis=1),
                jnp.concatenate(parts[i : i + 2], axis=0),
                preferred_element_type=F32,
            )
            both = part if both is None else both + part
        updates.append((load_ref[b] - split_product(both)).astype(BF16))
    for b, update in zip(blocks, updates):
        yield b, lam_ref[b] + complex_product(prec_ref[b], update)


def sweep_edge_kernel(
    parity_ref, cols_ref, from_other, from_partner, load_ref, lam_ref, diag_ref, off_ref, prec_ref,
    _, ext_ref, other_ref, partner_ref,
):
    nb = load_ref.shape[0]
    take_edges(parity_ref[0], from_other, from_partner, ext_ref)
    tiles = (diag_ref, off_ref, prec_ref)
    edges = [lam for _, lam in sweep_blocks((0, nb - 1), cols_ref, ext_ref, load_ref, lam_ref, *tiles)]
    send_edges(parity_ref[0], *edges, other_ref, partner_ref)


def sweep_kernel(
    cols_ref, ext_ref, load_ref, lam_ref, diag_ref, off_ref, prec_ref, lam_out, ext_out
):
    blocks, tiles = range(load_ref.shape[0]), (diag_ref, off_ref, prec_ref)
    for b, lam in sweep_blocks(blocks, cols_ref, ext_ref, load_ref, lam_ref, *tiles):
        lam_out[b] = lam
        ext_out[b + 1] = lam.astype(BF16)


def last_kernel(
    scale, parity_ref, cols_ref, from_other, from_partner, load_ref, lam_ref, diag_ref, off_ref,
    prec_ref, stiff_ref, _, adj_out, grad_out, ext_ref, part_ref,
):
    nb, m, cols = load_ref.shape
    half = cols // 2
    take_edges(parity_ref[0], from_other, from_partner, ext_ref)
    part_ref[...] = jnp.zeros_like(part_ref)
    tiles = (diag_ref, off_ref, prec_ref)
    for b, lam in sweep_blocks(range(nb), cols_ref, ext_ref, load_ref, lam_ref, *tiles):
        adj_out[b] = lam.astype(BF16)
        terms = lam * stiff_ref[b]
        part_ref[b : b + 1] = jnp.sum(terms[:, :half] + terms[:, half:], axis=0, keepdims=True)
    total = jnp.sum(jnp.transpose(part_ref[...]), axis=0, keepdims=True)
    grad_out[...] = total[:, :nb] * scale


IN_VMEM = pl.BlockSpec(memory_space=pltpu.VMEM)
IN_SMEM = pl.BlockSpec(memory_space=pltpu.SMEM)


def call(kernel, outs, ins, out_specs=None, scratch=(), aliases=None, mflops=1):
    return pl.pallas_call(
        kernel,
        out_shape=outs,
        in_specs=ins,
        out_specs=out_specs or tuple([IN_VMEM] * len(outs)),
        scratch_shapes=list(scratch),
        input_output_aliases=aliases or {},
        compiler_params=pltpu.CompilerParams(vmem_limit_bytes=VMEM_LIMIT),
        cost_estimate=pl.CostEstimate(
            flops=mflops * 1000000, bytes_accessed=4000000, transcendentals=0
        ),
    )


def swap_edges(to_other, to_partner, axis):
    count = lax.axis_size(axis)
    pairs = [(i, i ^ 1) for i in range(count)]
    others = [(i, i - 1 if i % 2 == 0 else i + 1) for i in range(1, count - 1)]
    return lax.ppermute(to_other, axis, others), lax.ppermute(to_partner, axis, pairs)


def shards(
    response, measured, sensor_owner, sensor_row, adj_diag, adj_off, block_cols, precond, stiff_deriv
):
    resp = response[0]
    diag, off, prec = adj_diag[0], adj_off[0], precond[0]
    nb, m, cols = resp.shape
    peers = lax.axis_size("sub")
    sensors = sensor_owner.shape[0]
    shape = jax.ShapeDtypeStruct
    owner, row = sensor_owner.reshape(1, sensors), sensor_row.reshape(1, sensors)
    owner, row, rows_in, place_id = lax.optimization_barrier(
        (owner, row, measured[0], lax.axis_index("sub") & 1)
    )
    near = block_cols.T
    numbers = pltpu.VMEM((1, sensors), jnp.int32)
    (packed,) = call(
        functools.partial(pack_kernel, m),
        (shape((2 * peers, (SLOTS + 1) * cols // 2), BF16),),
        [pl.BlockSpec(memory_space=pltpu.HBM)] * 3,
        scratch=[numbers, numbers, pltpu.VMEM((sensors, cols), BF16), pltpu.SemaphoreType.DMA((3,))],
    )(*(pltpu.with_memory_space_constraint(x, pltpu.HBM) for x in (owner, row, rows_in)))
    recv = lax.all_to_all(
        packed.reshape(peers, 2, -1), "sub", 0, 0, tiled=True
    ).reshape(packed.shape)
    parity = place_id.astype(jnp.int32).reshape(1)

    whole32, whole16 = shape((nb, m, cols), F32), shape((nb, m, cols), BF16)
    wide16, edge = shape((nb + 2, m, cols), BF16), shape((m, cols), BF16)
    place, rows, to_other, to_partner = call(
        edge_kernel,
        (shape((m, peers * SLOTS), jnp.int32), shape((peers * SLOTS, cols), BF16), edge, edge),
        [IN_SMEM] + [IN_VMEM] * 3,
        scratch=[pltpu.VMEM((2 * peers, cols // 2), F32)],
    )(parity, recv, resp, prec)
    from_other, from_partner = swap_edges(to_other, to_partner, "sub")
    load, lam, ext, stiff_resp = call(
        load_kernel, (whole32, whole32, wide16, whole32), [IN_VMEM] * 5, mflops=2000
    )(place, rows, resp, prec, stiff_deriv)

    ext, to_other, to_partner = call(
        sweep_edge_kernel,
        (wide16, edge, edge),
        [IN_SMEM, IN_VMEM] + [IN_VMEM] * 8,
        aliases={9: 0},
    )(parity, near, from_other, from_partner, load, lam, diag, off, prec, ext)
    from_other, from_partner = swap_edges(to_other, to_partner, "sub")
    lam, ext = call(sweep_kernel, (whole32, wide16), [IN_VMEM] + [IN_VMEM] * 6, mflops=2000)(
        near, ext, load, lam, diag, off, prec
    )

    scale = 1.0 / math.sqrt(m * cols)
    adjoint, grad, _ = call(
        functools.partial(last_kernel, scale),
        (whole16, shape((1, nb), F32), wide16),
        [IN_SMEM, IN_VMEM] + [IN_VMEM] * 9,
        scratch=[pltpu.VMEM((128, 128), F32)],
        aliases={10: 2},
    )(parity, near, from_other, from_partner, load, lam, diag, off, prec, stiff_resp, ext)
    gradient = lax.psum(grad.reshape(nb), "freq")
    return (adjoint[None], gradient)


def solution(mesh):
    in_specs = (
        P("freq", "sub", None, None),
        P("freq", "sub", None),
        P("sub"),
        P("sub"),
        P("freq", "sub", None, None, None),
        P("freq", "sub", None, None, None, None),
        P("sub", None),
        P("freq", "sub", None, None, None),
        P("sub", None, None),
    )
    out_specs = (P("freq", "sub", None, None), P("sub"))
    return jax.shard_map(shards, mesh=mesh, in_specs=in_specs, out_specs=out_specs, check_vma=False)
```
